32 devices in a mesh: boot: 2 (over x), samp: 16 (over z, y, core).
Axes of the slice: x: 2, y: 2, z: 4, core: 2. Of those that a mesh axis runs over, the one named last changes fastest.
Arguments:
- dosage: bfloat16 [32384, 512], P('samp'), may hold values from 0 to 2, as said below
- residuals: bfloat16 [32384, 1280], P('samp', 'boot'), may hold values from -300 to 300
- maf_bin: int32 [512], replicated, may hold values from 0 to 63
- gene_map: int32 [512], replicated, may hold values from 0 to 31, never falling along the last dimension, each value on 1 to 32 neighbouring positions
- gene_order: int32 [32], replicated, may hold values from 0 to 31, each once
Outputs:
- calibrated: float32 [32, 1280], P('samp', 'boot')
The draws below stay inside these ranges and needn't reach their ends.
Inputs may be any that keep to these rules, and one draw needn't show every extreme that they name: `dosage`: allele counts 0, 1 or 2. `gene_map`: never falling along the variants; each gene holds 1 to 32 consecutive variants, one gene exactly 32. `gene_order`: each gene once.
All inputs are finite; a program needn't handle non-finite values.
Results may differ from the reference program's by a relative error of at most 0.0003.
Values sent between devices are 32-bit elements; how exact they have to be, the bound alone decides.
A program may use at most 64 MiB of HBM per device.

```python
import math
import jax
import jax.numpy as jnp
import numpy as np
from jax import lax

S_DEV = 2024
GMAX = 32
RHOS = 11
MAF_BINS = 64
PERSON_TOTAL = 32384
BOOTS = 1280
LOCUS_TOTAL = 512
GENES = 32
N_SAMP = 16


def draw_dosage(key, part):
    seed_for_share, seed_leading, seed_trailing = jax.random.split(key, 3)
    minor_allele_share = jnp.exp(jax.random.uniform(seed_for_share, (LOCUS_TOTAL,), jnp.float32, jnp.log(0.005), jnp.log(0.05)))
    maternal_strand = jax.random.uniform(seed_leading, (PERSON_TOTAL, LOCUS_TOTAL), jnp.float32) < minor_allele_share[None, :]
    paternal_strand = jax.random.uniform(seed_trailing, (PERSON_TOTAL, LOCUS_TOTAL), jnp.float32) < minor_allele_share[None, :]
    return (maternal_strand.astype(jnp.float32) + paternal_strand.astype(jnp.float32)).astype(jnp.bfloat16)


def draw_residuals(key, part):
    key_noise, key_scale = jax.random.split(key, 2)
    position = jnp.arange(BOOTS, dtype=jnp.float32) / (BOOTS - 1)
    column_scale = jnp.exp(jnp.log(3.0) * position) * jnp.exp(jax.random.uniform(key_scale, (BOOTS,), jnp.float32, 0.0, jnp.log(4.0)))
    drawn = jax.random.normal(key_noise, (PERSON_TOTAL, BOOTS), jnp.float32) * column_scale[None, :]
    return jnp.clip(drawn, -300.0, 300.0).astype(jnp.bfloat16)


def set_ends(values, stream_key, least, high):
    spot = [jax.random.randint(jax.random.fold_in(stream_key, axis), (), 0, length) for axis, length in enumerate(values.shape)]
    main_axis = values.shape.index(max(values.shape))
    beside = spot[:main_axis] + [(spot[main_axis] + 1) % values.shape[main_axis]] + spot[main_axis + 1:]
    return values.at[tuple(spot)].set(least).at[tuple(beside)].set(high)


def split_up(number_of, total, limit, skew):
    weights = [(1 << 20) // math.isqrt(rank ** skew) + 1 for rank in range(2, number_of + 1)]
    rest, given = total - limit - (number_of - 1), [1] * (number_of - 1)
    while rest > 0:
        candidates = [i for i in range(number_of - 1) if given[i] < limit]
        mass, remaining = sum([weights[i] for i in candidates]), rest
        for i in candidates:
            more = min(limit - given[i], max(1, remaining * weights[i] // mass), rest)
            given[i] = given[i] + more
            rest = rest - more
    return np.array([limit] + given)


def ragged_sizes(rng, count, total, reach, slope):
    if count == 2:
        one = jax.random.randint(rng, (), max(1, total - reach), min(reach, total - 1) + 1)
        return jnp.stack([one, total - one])
    sizes = jnp.asarray(split_up(count, total, reach, slope), jnp.int32)
    couples = (count - 1) // 2
    giver, taker = sizes[1:1 + 2 * couples:2], sizes[2:2 + 2 * couples:2]
    room = jnp.minimum(giver - 1, reach - taker)
    moved = jax.random.randint(jax.random.fold_in(rng, 1), (couples,), 0, 1 << 20) % (room + 1)
    sizes = sizes.at[1:1 + 2 * couples:2].set(giver - moved).at[2:2 + 2 * couples:2].set(taker + moved)
    return sizes[jax.random.permutation(jax.random.fold_in(rng, 2), count)]


def setup_inputs(seed: int = 0) -> dict:
    seeds = jax.random.split(jax.random.key(seed), 6)
    dosage = draw_dosage(jax.random.fold_in(seeds[5], 71), 0)
    residuals = draw_residuals(jax.random.fold_in(seeds[5], 71), 0)
    maf_bin = set_ends(jax.random.randint(seeds[2], (LOCUS_TOTAL,), 0, MAF_BINS), jax.random.fold_in(seeds[2], 1), 0, MAF_BINS - 1).astype(jnp.int32)
    gene_map = jnp.searchsorted(jnp.cumsum(ragged_sizes(seeds[3], GENES, LOCUS_TOTAL, GMAX, 2)), jnp.arange(LOCUS_TOTAL), side="right").astype(jnp.int32)
    gene_order = jax.random.permutation(seeds[4], GENES).astype(jnp.int32)
    return {"dosage": dosage, "residuals": residuals, "maf_bin": maf_bin, "gene_map": gene_map, "gene_order": gene_order}


EPSILON = 1e-05

def variant_weights(maf_bin):
    levels = jnp.arange(MAF_BINS, dtype=jnp.float32)
    weight_table = (1.0 - 0.05 * (levels + 0.5) / MAF_BINS) ** 24
    matches = maf_bin[:, None] == jnp.arange(MAF_BINS, dtype=jnp.int32)[None, :]
    return lax.optimization_barrier(jnp.sum(jnp.where(matches, weight_table[None, :], jnp.zeros_like(weight_table)[None, :]), axis=1))

def reference(dosage, residuals, maf_bin, gene_map, gene_order):
    weights = variant_weights(maf_bin) / math.sqrt(PERSON_TOTAL)
    dose_blocks = dosage.reshape(N_SAMP, S_DEV, LOCUS_TOTAL)
    resid_blocks = residuals.reshape(N_SAMP, S_DEV, BOOTS)

    def add_block(running, block_pair):
        dose_block, resid_block = block_pair
        product = jnp.dot(dose_block.astype(jnp.float32).T, resid_block.astype(jnp.float32), precision=lax.Precision.HIGHEST)
        return (running + product, None)
    raw_scores, _ = lax.scan(add_block, jnp.zeros((LOCUS_TOTAL, BOOTS), jnp.float32), (dose_blocks, resid_blocks))
    scores = raw_scores * weights[:, None]
    burden = jax.ops.segment_sum(scores, gene_map, GENES)[gene_order]
    skat = jax.ops.segment_sum(scores * scores, gene_map, GENES)[gene_order]
    rho_grid = jnp.arange(RHOS, dtype=jnp.float32) / (RHOS - 1)
    mixtures = (1.0 - rho_grid)[None, :, None] * skat[:, None, :] + rho_grid[None, :, None] * (burden * burden)[:, None, :]
    center = lax.optimization_barrier(jnp.mean(mixtures, axis=2, keepdims=True))
    deviation = mixtures - center
    spread = lax.optimization_barrier(jnp.mean(deviation * deviation, axis=2, keepdims=True))
    zscore = deviation / jnp.sqrt(spread + EPSILON)
    return lax.optimization_barrier(jnp.max(zscore, axis=1))
```

```python
import functools

import jax
import jax.numpy as jnp
from jax import lax
from jax.experimental import pallas as pl
from jax.experimental.pallas import tpu as pltpu
from jax.sharding import PartitionSpec as P

RHOS = 11
MAF_BINS = 64
EPSILON = 1e-05
CHUNKS = 4
MESH = pl.DeviceIdType.MESH


def up(value, unit):
    return (value + unit - 1) // unit * unit


def kernel(
    n_boot,
    n_samp,
    rows,
    half,
    dose_hbm,
    resid_hbm,
    maf_ref,
    map_ref,
    order_ref,
    out_ref,
    dose,
    resid,
    acc,
    *rest,
):
    levels = n_samp.bit_length() - 1
    landed = rest[:levels]
    stacked, block, gathered = rest[levels:levels + 3]
    load_sem, send_sem, recv_sem, spread_send, spread_recv = rest[levels + 3:]
    devices = n_boot * n_samp
    variants = dose.shape[1]
    width = variants // CHUNKS
    genes = order_ref.shape[1]
    gene_dev = genes // n_samp
    rows_p = acc.shape[2]
    my_boot = lax.axis_index("boot")
    me = lax.axis_index("samp")
    linear = my_boot * n_samp + me

    loads = [pltpu.make_async_copy(resid_hbm, resid, load_sem.at[0])]
    for c in range(CHUNKS):
        cols = pl.ds(c * width, width)
        loads.append(
            pltpu.make_async_copy(dose_hbm.at[:, cols], dose.at[:, cols], load_sem.at[1 + c])
        )
    for load in loads:
        load.start()

    barrier = pltpu.get_barrier_semaphore()

    def others(step):
        if devices <= 32:
            for o in range(1, devices):
                step(o)
        else:
            lax.fori_loop(1, devices, lambda o, carry: (step(o), carry)[1], 0)

    def target(o):
        other = lax.rem(linear + o, devices)
        return (other // n_samp, lax.rem(other, n_samp))

    def greet(o):
        pl.semaphore_signal(barrier, inc=1, device_id=target(o), device_id_type=MESH)

    others(greet)

    person_total = resid.shape[0] * n_samp
    base = 1.0 - 0.05 * (maf_ref[...].astype(jnp.float32) + 0.5) / MAF_BINS
    p2 = base * base
    p4 = p2 * p2
    p8 = p4 * p4
    weight = p8 * p8 * p8 / jnp.sqrt(jnp.full(base.shape, person_total, jnp.float32))
    order_row = order_ref[...].astype(jnp.float32)
    diagonal = lax.broadcasted_iota(jnp.int32, (genes, genes), 0) == lax.broadcasted_iota(
        jnp.int32, (genes, genes), 1
    )
    order_col = jnp.sum(
        jnp.where(diagonal, jnp.broadcast_to(order_row, (genes, genes)), 0.0), axis=1, keepdims=True
    )
    member = jnp.where(order_col == map_ref[...].astype(jnp.float32), 1.0, 0.0)

    bits = [lax.rem(me // (1 << t), 2) for t in range(levels)]
    lows, low = [], 0
    for t in range(levels):
        lows.append(low)
        low = low + bits[t] * (n_samp >> (t + 1))
    place = low

    def exchange(t, c):
        size = n_samp >> (t + 1)
        return pltpu.make_async_remote_copy(
            src_ref=acc.at[c, pl.ds(lows[t] + (1 - bits[t]) * size, size)],
            dst_ref=landed[t].at[c],
            send_sem=send_sem.at[t, c],
            recv_sem=recv_sem.at[t, c],
            device_id=(my_boot, me + (1 - 2 * bits[t]) * (1 << t)),
            device_id_type=MESH,
        )

    def product(c):
        loads[1 + c].wait()
        part = lax.dot_general(
            resid[...],
            dose[:, c * width:(c + 1) * width],
            (((0,), (0,)), ((), ())),
            preferred_element_type=jnp.float32,
        )
        if rows_p == rows:
            acc[c] = part.reshape(n_samp, rows, width)
        else:
            acc[c] = jnp.zeros((n_samp, rows_p, width), jnp.float32)
            for d in range(n_samp):
                acc[c, d, :rows] = part[d * rows:(d + 1) * rows]

    def fold(t, c):
        exchange(t, c).wait_recv()
        size = n_samp >> (t + 1)
        keep = pl.ds(lows[t] + bits[t] * size, size)
        acc[c, keep] = acc[c, keep] + landed[t][c]

    totals = []

    def genewise(c):
        span = slice(c * width, (c + 1) * width)
        scores = acc[c, pl.ds(place, 1)].reshape(rows_p, width) * weight[:, span]
        stacked[:rows_p] = scores * scores
        stacked[half:half + rows_p] = scores
        totals.append(
            lax.dot_general(
                member[:, span],
                stacked[...],
                (((1,), (1,)), ((), ())),
                precision=lax.Precision.HIGHEST,
                preferred_element_type=jnp.float32,
            )
        )

    stacked[...] = jnp.zeros(stacked.shape, jnp.float32)
    loads[0].wait()

    def after(t, c):
        fold(t, c)
        if t + 1 < levels:
            exchange(t + 1, c).start()
        else:
            genewise(c)

    for c in range(CHUNKS):
        product(c)
        if c == 0:
            pl.semaphore_wait(barrier, devices - 1)
        exchange(0, c).start()
        if c:
            after(0, c - 1)
    after(0, CHUNKS - 1)
    for wave in range(CHUNKS + levels - 2):
        for t in range(1, levels):
            c = wave - (t - 1)
            if 0 <= c < CHUNKS:
                after(t, c)

    total = functools.reduce(lambda a, b: a + b, totals)
    lane = lax.broadcasted_iota(jnp.int32, total.shape, 1)
    total = jnp.where(lane < half, total, total * total)
    for j in range(n_samp):
        block[j] = total[j * gene_dev:(j + 1) * gene_dev]

    slot = my_boot * n_samp + place

    def spread(o):
        there = target(o)
        pltpu.make_async_remote_copy(
            src_ref=block.at[there[1]],
            dst_ref=gathered.at[slot],
            send_sem=spread_send,
            recv_sem=spread_recv,
            device_id=there,
            device_id_type=MESH,
        ).start()

    others(spread)
    gathered[pl.ds(slot, 1)] = block[pl.ds(me, 1)]
    whole = gathered.at[pl.ds(0, devices - 1)]
    pltpu.make_async_copy(whole, whole, spread_recv).wait()

    count = float(devices * rows)
    mine = pl.ds(my_boot * n_samp, n_samp)
    for g in range(gene_dev):
        both = gathered[:, g, :]
        skat, square = both[:, :half], both[:, half:]
        own = gathered[mine, g, :]
        real = lax.broadcasted_iota(jnp.int32, skat.shape, 1) < rows
        skat_mean = jnp.sum(skat, keepdims=True) / count
        square_mean = jnp.sum(square, keepdims=True) / count
        skat_off = jnp.where(real, skat - skat_mean, 0.0)
        square_off = jnp.where(real, square - square_mean, 0.0)
        own_skat = own[:, :half] - skat_mean
        own_square = own[:, half:] - square_mean
        best = None
        for k in range(RHOS):
            rho = k / (RHOS - 1)
            off = (1.0 - rho) * skat_off + rho * square_off
            spread_k = jnp.sum(off * off, keepdims=True) / count
            score = ((1.0 - rho) * own_skat + rho * own_square) / jnp.sqrt(spread_k + EPSILON)
            best = score if best is None else jnp.maximum(best, score)
        out_ref[g] = best

    for t in range(levels):
        for c in range(CHUNKS):
            exchange(t, c).wait_send()
    pltpu.make_async_copy(whole, whole, spread_send).wait()


def shards(dosage, residuals, maf_bin, gene_map, gene_order):
    n_boot, n_samp = lax.axis_size("boot"), lax.axis_size("samp")
    samples, variants = dosage.shape
    boot_local = residuals.shape[1]
    genes = gene_order.shape[0]
    gene_dev = genes // n_samp
    rows = boot_local // n_samp
    rows_p = up(rows, 8)
    half = 64 if rows <= 64 else up(rows, 128)
    levels = n_samp.bit_length() - 1
    width = variants // CHUNKS
    vmem = pl.BlockSpec(memory_space=pltpu.VMEM)
    hbm = pl.BlockSpec(memory_space=pl.ANY)
    best = pl.pallas_call(
        functools.partial(kernel, n_boot, n_samp, rows, half),
        name="skato",
        out_shape=jax.ShapeDtypeStruct((gene_dev, n_samp, half), jnp.float32),
        in_specs=[hbm, hbm, vmem, vmem, vmem],
        out_specs=vmem,
        scratch_shapes=[
            pltpu.VMEM((samples, variants), jnp.bfloat16),
            pltpu.VMEM((samples, boot_local), jnp.bfloat16),
            pltpu.VMEM((CHUNKS, n_samp, rows_p, width), jnp.float32),
            *[
                pltpu.VMEM((CHUNKS, n_samp >> (t + 1), rows_p, width), jnp.float32)
                for t in range(levels)
            ],
            pltpu.VMEM((2 * half, width), jnp.float32),
            pltpu.VMEM((n_samp, gene_dev, 2 * half), jnp.float32),
            pltpu.VMEM((n_boot * n_samp, gene_dev, 2 * half), jnp.float32),
            pltpu.SemaphoreType.DMA((1 + CHUNKS,)),
            pltpu.SemaphoreType.DMA((levels, CHUNKS)),
            pltpu.SemaphoreType.DMA((levels, CHUNKS)),
            pltpu.SemaphoreType.DMA,
            pltpu.SemaphoreType.DMA,
        ],
        compiler_params=pltpu.CompilerParams(
            collective_id=0, has_side_effects=True, vmem_limit_bytes=60 * 1024 * 1024
        ),
    )(dosage, residuals, maf_bin[None, :], gene_map[None, :], gene_order[None, :])
    return best[:, :, :rows].reshape(gene_dev, boot_local)


def solution(mesh):
    placed = (P("samp", None), P("samp", "boot"), P(), P(), P())
    return jax.shard_map(
        shards, mesh=mesh, in_specs=placed, out_specs=P("samp", "boot"), check_vma=False
    )
```

```python
import functools
import math

import jax
import jax.numpy as jnp
from jax import lax
from jax.experimental import pallas as pl
from jax.experimental.pallas import tpu as pltpu
from jax.sharding import PartitionSpec as P

RHOS = 11
MAF_BINS = 64
EPSILON = 1e-05
MESH = pl.DeviceIdType.MESH


def up(value, unit):
    return (value + unit - 1) // unit * unit


def chunking(rows):
    for count in range(rows // 8, 0, -1):
        if rows % (8 * count) == 0:
            return count
    return 1


def bit_order(kind, levels):
    if kind == 0 or levels < 3:
        return tuple(range(levels))
    return (0, *range(2, levels), 1)


def place_of(samp, order):
    size = 1 << len(order)
    return sum((samp // (1 << bit) % 2) * (size >> (t + 1)) for t, bit in enumerate(order))


def schedule(kinds, levels):
    steps, turn = [], 0
    for c, kind in enumerate(kinds):
        if kind == 0:
            begin = 2.6 + 1.4 * turn
            turn += 1
            times = [begin + 2.6 * (t - 1) for t in range(1, levels)]
        else:
            times = [4.0 + 2.7 * (t - 1) for t in range(1, levels)]
        steps += [(time, t, c) for t, time in enumerate(times, 1)]
    return [(t, c) for _, t, c in sorted(steps)]


def kernel(
    n_boot,
    n_samp,
    rows,
    half,
    kinds,
    dose_hbm,
    resid_hbm,
    maf_ref,
    map_ref,
    order_ref,
    out_ref,
    dose,
    resid,
    acc,
    *rest,
):
    levels = n_samp.bit_length() - 1
    chunks = len(kinds)
    orders = [bit_order(kind, levels) for kind in kinds]
    landed = rest[:levels]
    stacked, block, gathered = rest[levels:levels + 3]
    load_sem, send_sem, recv_sem, spread_send, spread_recv = rest[levels + 3:]
    devices = n_boot * n_samp
    variants = dose.shape[1]
    width = resid.shape[1] // chunks
    genes = order_ref.shape[1]
    gene_dev = genes // n_samp
    rows_p = acc.shape[2]
    my_boot = lax.axis_index("boot")
    me = lax.axis_index("samp")
    linear = my_boot * n_samp + me
    bits = [lax.rem(me // (1 << t), 2) for t in range(levels)]
    partners = [me + (1 - 2 * bits[t]) * (1 << t) for t in range(levels)]

    loads = [pltpu.make_async_copy(dose_hbm, dose, load_sem.at[0])]
    for c in range(chunks):
        cols = pl.ds(c * width, width)
        loads.append(
            pltpu.make_async_copy(resid_hbm.at[:, cols], resid.at[:, cols], load_sem.at[1 + c])
        )
    for load in loads:
        load.start()

    barrier = pltpu.get_barrier_semaphore()
    for t in range(levels):
        pl.semaphore_signal(
            barrier, inc=1, device_id=(my_boot, partners[t]), device_id_type=MESH
        )
    for o in range(1, n_boot):
        pl.semaphore_signal(
            barrier, inc=1, device_id=(lax.rem(my_boot + o, n_boot), me), device_id_type=MESH
        )

    person_total = resid.shape[0] * n_samp
    base = 1.0 - 0.05 * (maf_ref[...].astype(jnp.float32) + 0.5) / MAF_BINS
    p2 = base * base
    p4 = p2 * p2
    p8 = p4 * p4
    weight = p8 * p8 * p8 / math.sqrt(person_total)
    order_row = order_ref[...].astype(jnp.float32)
    diagonal = lax.broadcasted_iota(jnp.int32, (genes, genes), 0) == lax.broadcasted_iota(
        jnp.int32, (genes, genes), 1
    )
    order_col = jnp.sum(
        jnp.where(diagonal, jnp.broadcast_to(order_row, (genes, genes)), 0.0), axis=1, keepdims=True
    )
    member = jnp.where(order_col == map_ref[...].astype(jnp.float32), 1.0, 0.0)

    lows, places = [], []
    for order in orders:
        low, line = 0, []
        for t, bit in enumerate(order):
            line.append(low)
            low = low + bits[bit] * (n_samp >> (t + 1))
        lows.append(line)
        places.append(low)
    natural = place_of(me, bit_order(0, levels))

    def exchange(t, c):
        size = n_samp >> (t + 1)
        bit = orders[c][t]
        return pltpu.make_async_remote_copy(
            src_ref=acc.at[c, pl.ds(lows[c][t] + (1 - bits[bit]) * size, size)],
            dst_ref=landed[t].at[c],
            send_sem=send_sem.at[t, c],
            recv_sem=recv_sem.at[t, c],
            device_id=(my_boot, partners[bit]),
            device_id_type=MESH,
        )

    def product(c):
        loads[1 + c].wait()
        part = lax.dot_general(
            resid[:, c * width:(c + 1) * width],
            dose[...],
            (((0,), (0,)), ((), ())),
            preferred_element_type=jnp.float32,
        )
        if rows_p != rows:
            acc[c] = jnp.zeros((n_samp, rows_p, variants), jnp.float32)
        for s in range(n_samp):
            n = place_of(s, bit_order(0, levels))
            acc[c, place_of(s, orders[c]), :rows] = part[n * rows:(n + 1) * rows]

    def fold(t, c):
        exchange(t, c).wait_recv()
        size = n_samp >> (t + 1)
        keep = pl.ds(lows[c][t] + bits[orders[c][t]] * size, size)
        acc[c, keep] = acc[c, keep] + landed[t][c]

    finished, totals = [], []

    def genewise(late):
        totals.append(
            lax.dot_general(
                member,
                stacked[late],
                (((1,), (1,)), ((), ())),
                precision=lax.Precision.HIGHEST,
                preferred_element_type=jnp.float32,
            )
        )

    def after(t, c):
        fold(t, c)
        if t + 1 < levels:
            exchange(t + 1, c).start()
            return
        scores = acc[c, pl.ds(places[c], 1)].reshape(rows_p, variants) * weight
        late = int(len(finished) == chunks - 1)
        finished.append(c)
        stacked[late, c * rows_p:(c + 1) * rows_p] = scores * scores
        stacked[late, half + c * rows_p:half + (c + 1) * rows_p] = scores
        if late or len(finished) == chunks - 1:
            genewise(late)

    stacked[...] = jnp.zeros(stacked.shape, jnp.float32)
    loads[0].wait()
    for c in range(chunks):
        product(c)
        if c == 0:
            pl.semaphore_wait(barrier, levels + n_boot - 1)
        exchange(0, c).start()
        if c:
            after(0, c - 1)
    after(0, chunks - 1)
    for t, c in schedule(kinds, levels):
        after(t, c)

    total = functools.reduce(lambda a, b: a + b, totals)
    lane = lax.broadcasted_iota(jnp.int32, total.shape, 1)
    total = jnp.where(lane < half, total, total * total)
    for j in range(n_samp):
        block[j] = total[j * gene_dev:(j + 1) * gene_dev]

    slot = my_boot * n_samp + natural

    def spread(o):
        other = lax.rem(linear + o, devices)
        there = (other // n_samp, lax.rem(other, n_samp))
        pltpu.make_async_remote_copy(
            src_ref=block.at[there[1]],
            dst_ref=gathered.at[slot],
            send_sem=spread_send,
            recv_sem=spread_recv,
            device_id=there,
            device_id_type=MESH,
        ).start()

    if devices <= 32:
        for o in range(1, devices):
            spread(o)
    else:
        lax.fori_loop(1, devices, lambda o, carry: (spread(o), carry)[1], 0)
    gathered[pl.ds(slot, 1)] = block[pl.ds(me, 1)]
    for t in range(levels):
        for c in range(chunks):
            exchange(t, c).wait_send()
    local = resid.shape[1]
    shape = (half, local)
    resample = lax.broadcasted_iota(jnp.int32, shape, 1)
    held = lax.div(resample, width) * rows_p + lax.rem(resample, rows)
    picked = jnp.where(held == lax.broadcasted_iota(jnp.int32, shape, 0), 1.0, 0.0)
    shape = (n_samp, local)
    resample = lax.broadcasted_iota(jnp.int32, shape, 1)
    owner = lax.div(lax.rem(resample, width), rows)
    owned = owner == lax.broadcasted_iota(jnp.int32, shape, 0)
    whole = gathered.at[pl.ds(0, devices - 1)]
    pltpu.make_async_copy(whole, whole, spread_recv).wait()

    count = float(devices * chunks * rows)
    mine = pl.ds(my_boot * n_samp, n_samp)
    for g in range(gene_dev):
        both = gathered[:, g, :]
        skat, square = both[:, :half], both[:, half:]
        own = gathered[mine, g, :]
        lane = lax.broadcasted_iota(jnp.int32, skat.shape, 1)
        real = (lax.rem(lane, rows_p) < rows) & (lane < chunks * rows_p)
        skat_mean = jnp.sum(skat, keepdims=True) / count
        square_mean = jnp.sum(square, keepdims=True) / count
        skat_off = jnp.where(real, skat - skat_mean, 0.0)
        square_off = jnp.where(real, square - square_mean, 0.0)
        own_skat = own[:, :half] - skat_mean
        own_square = own[:, half:] - square_mean
        best = None
        for k in range(RHOS):
            rho = k / (RHOS - 1)
            off = (1.0 - rho) * skat_off + rho * square_off
            spread_k = jnp.sum(off * off, keepdims=True) / count
            score = ((1.0 - rho) * own_skat + rho * own_square) / jnp.sqrt(spread_k + EPSILON)
            best = score if best is None else jnp.maximum(best, score)
        placed = lax.dot_general(
            best,
            picked,
            (((1,), (0,)), ((), ())),
            precision=lax.Precision.HIGHEST,
            preferred_element_type=jnp.float32,
        )
        out_ref[g:g + 1] = jnp.sum(jnp.where(owned, placed, 0.0), axis=0, keepdims=True)

    pltpu.make_async_copy(whole, whole, spread_send).wait()


def shards(dosage, residuals, maf_bin, gene_map, gene_order):
    n_boot, n_samp = lax.axis_size("boot"), lax.axis_size("samp")
    samples, variants = dosage.shape
    boot_local = residuals.shape[1]
    genes = gene_order.shape[0]
    gene_dev = genes // n_samp
    chunks = chunking(boot_local // n_samp)
    rows = boot_local // n_samp // chunks
    rows_p = up(rows, 8)
    half = 64 if chunks * rows_p <= 64 else up(chunks * rows_p, 128)
    levels = n_samp.bit_length() - 1
    kinds = tuple(int(c in (1, 3)) for c in range(chunks))
    vmem = pl.BlockSpec(memory_space=pltpu.VMEM)
    hbm = pl.BlockSpec(memory_space=pl.ANY)
    return pl.pallas_call(
        functools.partial(kernel, n_boot, n_samp, rows, half, kinds),
        name="skato",
        out_shape=jax.ShapeDtypeStruct((gene_dev, boot_local), jnp.float32),
        in_specs=[hbm, hbm, vmem, vmem, vmem],
        out_specs=vmem,
        scratch_shapes=[
            pltpu.VMEM((samples, variants), jnp.bfloat16),
            pltpu.VMEM((samples, boot_local), jnp.bfloat16),
            pltpu.VMEM((chunks, n_samp, rows_p, variants), jnp.float32),
            *[
                pltpu.VMEM((chunks, n_samp >> (t + 1), rows_p, variants), jnp.float32)
                for t in range(levels)
            ],
            pltpu.VMEM((2, 2 * half, variants), jnp.float32),
            pltpu.VMEM((n_samp, gene_dev, 2 * half), jnp.float32),
            pltpu.VMEM((n_boot * n_samp, gene_dev, 2 * half), jnp.float32),
            pltpu.SemaphoreType.DMA((1 + chunks,)),
            pltpu.SemaphoreType.DMA((levels, chunks)),
            pltpu.SemaphoreType.DMA((levels, chunks)),
            pltpu.SemaphoreType.DMA,
            pltpu.SemaphoreType.DMA,
        ],
        compiler_params=pltpu.CompilerParams(
            collective_id=0, has_side_effects=True, vmem_limit_bytes=60 * 1024 * 1024
        ),
    )(dosage, residuals, maf_bin[None, :], gene_map[None, :], gene_order[None, :])


def solution(mesh):
    placed = (P("samp", None), P("samp", "boot"), P(), P(), P())
    return jax.shard_map(
        shards, mesh=mesh, in_specs=placed, out_specs=P("samp", "boot"), check_vma=False
    )
```

```python
import functools
import math

import jax
import jax.numpy as jnp
from jax import lax
from jax.experimental import pallas as pl
from jax.experimental.pallas import tpu as pltpu
from jax.sharding import PartitionSpec as P

RHOS = 11
MAF_BINS = 64
EPSILON = 1e-05
MESH = pl.DeviceIdType.MESH


def up(value, unit):
    return (value + unit - 1) // unit * unit


def chunking(rows):
    for count in range(rows // 8, 0, -1):
        if rows % (8 * count) == 0:
            return count
    return 1


def phases_of(levels):
    groups = [(bit,) for bit in range(min(2, levels))]
    bit = 2
    while bit < levels:
        groups.append(tuple(range(bit, min(bit + 2, levels))))
        bit += 2
    return groups


def schedule(chunks, phases):
    steps = [
        (2.6 + 1.4 * c + 3.5 * (t - 1), t, c) for c in range(chunks) for t in range(1, phases)
    ]
    return [(t, c) for _, t, c in sorted(steps)]


def kernel(
    n_boot,
    n_samp,
    rows,
    half,
    chunks,
    dose_hbm,
    resid_hbm,
    maf_ref,
    map_ref,
    order_ref,
    out_ref,
    dose,
    resid,
    acc,
    *rest,
):
    levels = n_samp.bit_length() - 1
    groups = phases_of(levels)
    phases = len(groups)
    landed = rest[:phases]
    stacked, block, gathered = rest[phases:phases + 3]
    load_sem, send_sem, recv_sem, spread_send, spread_recv = rest[phases + 3:]
    devices = n_boot * n_samp
    variants = dose.shape[1]
    width = resid.shape[1] // chunks
    genes = order_ref.shape[1]
    gene_dev = genes // n_samp
    rows_p = acc.shape[2]
    my_boot = lax.axis_index("boot")
    me = lax.axis_index("samp")
    linear = my_boot * n_samp + me
    bits = [lax.rem(me // (1 << t), 2) for t in range(levels)]
    flips = [(1 - 2 * bits[t]) * (1 << t) for t in range(levels)]
    moves = [list(range((1 << len(group)) - 1, 0, -1)) for group in groups]

    def partner(t, move):
        return me + sum(flips[bit] for i, bit in enumerate(groups[t]) if move >> i & 1)

    def digit(t, move):
        return sum(
            ((1 - bits[bit]) if move >> i & 1 else bits[bit]) * (1 << (len(groups[t]) - 1 - i))
            for i, bit in enumerate(groups[t])
        )

    sizes, lows, low, size = [], [], 0, n_samp
    for t, group in enumerate(groups):
        size >>= len(group)
        sizes.append(size)
        lows.append(low)
        low = low + digit(t, 0) * size
    natural = low

    loads = [pltpu.make_async_copy(dose_hbm, dose, load_sem.at[0])]
    for c in range(chunks):
        cols = pl.ds(c * width, width)
        loads.append(
            pltpu.make_async_copy(resid_hbm.at[:, cols], resid.at[:, cols], load_sem.at[1 + c])
        )
    for load in loads:
        load.start()

    barrier = pltpu.get_barrier_semaphore()
    for t in range(phases):
        for move in moves[t]:
            pl.semaphore_signal(
                barrier, inc=1, device_id=(my_boot, partner(t, move)), device_id_type=MESH
            )
    for o in range(1, n_boot):
        pl.semaphore_signal(
            barrier, inc=1, device_id=(lax.rem(my_boot + o, n_boot), me), device_id_type=MESH
        )

    person_total = resid.shape[0] * n_samp
    base = 1.0 - 0.05 * (maf_ref[...].astype(jnp.float32) + 0.5) / MAF_BINS
    p2 = base * base
    p4 = p2 * p2
    p8 = p4 * p4
    weight = p8 * p8 * p8 / math.sqrt(person_total)
    order_row = order_ref[...].astype(jnp.float32)
    diagonal = lax.broadcasted_iota(jnp.int32, (genes, genes), 0) == lax.broadcasted_iota(
        jnp.int32, (genes, genes), 1
    )
    order_col = jnp.sum(
        jnp.where(diagonal, jnp.broadcast_to(order_row, (genes, genes)), 0.0), axis=1, keepdims=True
    )
    member = jnp.where(order_col == map_ref[...].astype(jnp.float32), 1.0, 0.0)

    def exchange(t, c, move):
        return pltpu.make_async_remote_copy(
            src_ref=acc.at[c, pl.ds(lows[t] + digit(t, move) * sizes[t], sizes[t])],
            dst_ref=landed[t].at[c, move - 1],
            send_sem=send_sem.at[t, c, move - 1],
            recv_sem=recv_sem.at[t, c, move - 1],
            device_id=(my_boot, partner(t, move)),
            device_id_type=MESH,
        )

    def send(t, c):
        for move in moves[t]:
            exchange(t, c, move).start()

    def product(c):
        loads[1 + c].wait()
        part = lax.dot_general(
            resid[:, c * width:(c + 1) * width],
            dose[...],
            (((0,), (0,)), ((), ())),
            preferred_element_type=jnp.float32,
        )
        if rows_p != rows:
            acc[c] = jnp.zeros((n_samp, rows_p, variants), jnp.float32)
            for n in range(n_samp):
                acc[c, n, :rows] = part[n * rows:(n + 1) * rows]
        else:
            acc[c] = part.reshape(n_samp, rows, variants)

    def fold(t, c):
        keep = pl.ds(lows[t] + digit(t, 0) * sizes[t], sizes[t])
        running = acc[c, keep]
        for move in reversed(moves[t]):
            exchange(t, c, move).wait_recv()
            running = running + landed[t][c, move - 1]
        acc[c, keep] = running

    finished, totals = [], []

    def genewise(late):
        totals.append(
            lax.dot_general(
                member,
                stacked[late],
                (((1,), (1,)), ((), ())),
                precision=lax.Precision.HIGHEST,
                preferred_element_type=jnp.float32,
            )
        )

    def after(t, c):
        fold(t, c)
        if t + 1 < phases:
            send(t + 1, c)
            return
        scores = acc[c, pl.ds(natural, 1)].reshape(rows_p, variants) * weight
        late = int(len(finished) == chunks - 1)
        finished.append(c)
        stacked[late, c * rows_p:(c + 1) * rows_p] = scores * scores
        stacked[late, half + c * rows_p:half + (c + 1) * rows_p] = scores
        if late or len(finished) == chunks - 1:
            genewise(late)

    stacked[...] = jnp.zeros(stacked.shape, jnp.float32)
    loads[0].wait()
    for c in range(chunks):
        product(c)
        if c == 0:
            pl.semaphore_wait(barrier, sum(len(m) for m in moves) + n_boot - 1)
        send(0, c)
        if c:
            after(0, c - 1)
    after(0, chunks - 1)
    for t, c in schedule(chunks, phases):
        after(t, c)

    total = functools.reduce(lambda a, b: a + b, totals)
    lane = lax.broadcasted_iota(jnp.int32, total.shape, 1)
    total = jnp.where(lane < half, total, total * total)
    for j in range(n_samp):
        block[j] = total[j * gene_dev:(j + 1) * gene_dev]

    slot = my_boot * n_samp + natural

    def spread_to(boot, samp):
        pltpu.make_async_remote_copy(
            src_ref=block.at[samp],
            dst_ref=gathered.at[slot],
            send_sem=spread_send,
            recv_sem=spread_recv,
            device_id=(boot, samp),
            device_id_type=MESH,
        ).start()

    def spread(o):
        other = lax.rem(linear + o, devices)
        spread_to(other // n_samp, lax.rem(other, n_samp))

    if devices <= 32:
        boots = [lax.rem(my_boot + o, n_boot) for o in range(n_boot)]
        flipped, there = (1 << levels) - 1, me + sum(flips)
        for i in range(n_samp):
            for o in range(n_boot - 1, -1, -1):
                if o or flipped:
                    spread_to(boots[o], there)
            if i + 1 < n_samp:
                bit = ((i + 1) & -(i + 1)).bit_length() - 1
                there = there - flips[bit] if flipped >> bit & 1 else there + flips[bit]
                flipped ^= 1 << bit
    else:
        lax.fori_loop(1, devices, lambda o, carry: (spread(o), carry)[1], 0)
    gathered[pl.ds(slot, 1)] = block[pl.ds(me, 1)]
    for t in range(phases):
        for c in range(chunks):
            for move in moves[t]:
                exchange(t, c, move).wait_send()
    local = resid.shape[1]
    shape = (half, local)
    resample = lax.broadcasted_iota(jnp.int32, shape, 1)
    held = lax.div(resample, width) * rows_p + lax.rem(resample, rows)
    picked = jnp.where(held == lax.broadcasted_iota(jnp.int32, shape, 0), 1.0, 0.0)
    shape = (n_samp, local)
    resample = lax.broadcasted_iota(jnp.int32, shape, 1)
    owner = lax.div(lax.rem(resample, width), rows)
    owned = owner == lax.broadcasted_iota(jnp.int32, shape, 0)
    whole = gathered.at[pl.ds(0, devices - 1)]
    pltpu.make_async_copy(whole, whole, spread_recv).wait()

    count = float(devices * chunks * rows)
    mine = pl.ds(my_boot * n_samp, n_samp)
    for g in range(gene_dev):
        both = gathered[:, g, :]
        skat, square = both[:, :half], both[:, half:]
        own = gathered[mine, g, :]
        lane = lax.broadcasted_iota(jnp.int32, skat.shape, 1)
        real = (lax.rem(lane, rows_p) < rows) & (lane < chunks * rows_p)
        skat_mean = jnp.sum(skat, keepdims=True) / count
        square_mean = jnp.sum(square, keepdims=True) / count
        skat_off = jnp.where(real, skat - skat_mean, 0.0)
        square_off = jnp.where(real, square - square_mean, 0.0)
        own_skat = own[:, :half] - skat_mean
        own_square = own[:, half:] - square_mean
        best = None
        for k in range(RHOS):
            rho = k / (RHOS - 1)
            off = (1.0 - rho) * skat_off + rho * square_off
            spread_k = jnp.sum(off * off, keepdims=True) / count
            score = ((1.0 - rho) * own_skat + rho * own_square) / jnp.sqrt(spread_k + EPSILON)
            best = score if best is None else jnp.maximum(best, score)
        placed = lax.dot_general(
            best,
            picked,
            (((1,), (0,)), ((), ())),
            precision=lax.Precision.HIGHEST,
            preferred_element_type=jnp.float32,
        )
        out_ref[g:g + 1] = jnp.sum(jnp.where(owned, placed, 0.0), axis=0, keepdims=True)

    pltpu.make_async_copy(whole, whole, spread_send).wait()


def shards(dosage, residuals, maf_bin, gene_map, gene_order):
    n_boot, n_samp = lax.axis_size("boot"), lax.axis_size("samp")
    samples, variants = dosage.shape
    boot_local = residuals.shape[1]
    genes = gene_order.shape[0]
    gene_dev = genes // n_samp
    chunks = chunking(boot_local // n_samp)
    rows = boot_local // n_samp // chunks
    rows_p = up(rows, 8)
    half = 64 if chunks * rows_p <= 64 else up(chunks * rows_p, 128)
    levels = n_samp.bit_length() - 1
    groups = phases_of(levels)
    fan = max(len(group) for group in groups)
    taken = [sum(len(group) for group in groups[:t + 1]) for t in range(len(groups))]
    vmem = pl.BlockSpec(memory_space=pltpu.VMEM)
    hbm = pl.BlockSpec(memory_space=pl.ANY)
    return pl.pallas_call(
        functools.partial(kernel, n_boot, n_samp, rows, half, chunks),
        name="skato",
        out_shape=jax.ShapeDtypeStruct((gene_dev, boot_local), jnp.float32),
        in_specs=[hbm, hbm, vmem, vmem, vmem],
        out_specs=vmem,
        scratch_shapes=[
            pltpu.VMEM((samples, variants), jnp.bfloat16),
            pltpu.VMEM((samples, boot_local), jnp.bfloat16),
            pltpu.VMEM((chunks, n_samp, rows_p, variants), jnp.float32),
            *[
                pltpu.VMEM(
                    (chunks, (1 << len(group)) - 1, n_samp >> bits, rows_p, variants), jnp.float32
                )
                for group, bits in zip(groups, taken)
            ],
            pltpu.VMEM((2, 2 * half, variants), jnp.float32),
            pltpu.VMEM((n_samp, gene_dev, 2 * half), jnp.float32),
            pltpu.VMEM((n_boot * n_samp, gene_dev, 2 * half), jnp.float32),
            pltpu.SemaphoreType.DMA((1 + chunks,)),
            pltpu.SemaphoreType.DMA((len(groups), chunks, (1 << fan) - 1)),
            pltpu.SemaphoreType.DMA((len(groups), chunks, (1 << fan) - 1)),
            pltpu.SemaphoreType.DMA,
            pltpu.SemaphoreType.DMA,
        ],
        compiler_params=pltpu.CompilerParams(
            collective_id=0, has_side_effects=True, vmem_limit_bytes=60 * 1024 * 1024
        ),
    )(dosage, residuals, maf_bin[None, :], gene_map[None, :], gene_order[None, :])


def solution(mesh):
    placed = (P("samp", None), P("samp", "boot"), P(), P(), P())
    return jax.shard_map(
        shards, mesh=mesh, in_specs=placed, out_specs=P("samp", "boot"), check_vma=False
    )
```
